32 devices in a mesh: port: 4 (over x, core), fac: 4 (over z), scen: 2 (over y).
Axes of the slice: x: 2, y: 2, z: 4, core: 2. Of those that a mesh axis runs over, the one named last changes fastest.
Arguments:
- shocks: bfloat16 [4096, 16384], P(('port', 'scen'), 'fac'), may hold values from -6 to 6
- loading: bfloat16 [16384, 8192], P('fac', 'port'), may hold values from -0.046875 to 0.046875
- thresholds: float32 [64, 8192], P(None, 'port'), may hold values from -1 to 3.5
- weights: bfloat16 [4096], P(('port', 'scen')), may hold values from 0.5 to 5, as said below
Outputs:
- mean_excess: float32 [64, 8192], P(None, 'port')
- tail_prob: float32 [64, 8192], P(None, 'port')
The draws below stay inside these ranges and needn't reach their ends.
Inputs may be any that keep to these rules, and one draw needn't show every extreme that they name: Positive weights.
All inputs are finite; a program needn't handle non-finite values.
Results may differ from the reference program's by a relative error of at most 0.008.
Values may be sent and summed in bfloat16 or wider, within the bound.
No kernel may reach another device: no remote copies, remote signals or barrier semaphores. Data moves between devices by JAX's collectives and lax.ppermute only.
A program may use at most 128 MiB of HBM per device.

```python
import jax
import jax.numpy as jnp
from jax import lax

FACTORS = 16384
PORTFOLIOS = 8192
LEVELS = 64
SCENARIOS = 4096
N_FAC = 4


def draw_weights(key, part):
    index = jnp.arange(SCENARIOS).astype(jnp.float32)
    base = jnp.exp(jnp.log(3.0) * index / SCENARIOS)
    noise = jnp.exp(jax.random.uniform(key, (SCENARIOS,), jnp.float32, -0.4, 0.4))
    return (base * noise).astype(jnp.bfloat16)


def block_scale(own_key, extent, cuts, least, high):
    def one(axis_at, blocks):
        draws = jax.random.uniform(jax.random.fold_in(jax.random.fold_in(own_key, 6), axis_at), (blocks,), jnp.float32, least / len(cuts), high / len(cuts))
        return jnp.repeat(jnp.exp(draws), extent[axis_at] // blocks).reshape((-1,) + (1,) * (len(extent) - axis_at - 1))

    level = one(*cuts[0])
    for cut in cuts[1:]:
        level = level * one(*cut)
    return level


def scatter_about(own_key, extent, width, bound, shards=(), held_as=jnp.bfloat16):
    drawn = width * jax.random.normal(own_key, extent, jnp.float32)
    if shards:
        drawn = drawn * block_scale(own_key, extent, shards, -0.22, 0.18)
    return jnp.clip(drawn, -bound, bound).astype(held_as)


def setup_inputs(seed: int = 0) -> dict:
    key_of = jax.random.split(jax.random.key(seed), 5)
    return {
        "shocks": scatter_about(key_of[0], (SCENARIOS, FACTORS), 1.0, 6.0, ((0, 8), (1, 4))),
        "loading": scatter_about(key_of[1], (FACTORS, PORTFOLIOS), FACTORS ** -0.5, 0.046875, ((0, 4), (1, 4))),
        "thresholds": jnp.clip(-1.0 + 4.5 * jax.random.uniform(key_of[2], (LEVELS, PORTFOLIOS), jnp.float32) ** block_scale(key_of[2], (LEVELS, PORTFOLIOS), ((1, 4),), -0.2, 0.2), -1.0, 3.5),
        "weights": draw_weights(jax.random.fold_in(key_of[4], 71), 0),
    }


smooth_width = 0.05


def reference(shocks, loading, thresholds, weights):
    fac_width = FACTORS // N_FAC

    def add_block(running, index):
        start = (index * fac_width).astype(jnp.int32)
        shock_block = lax.dynamic_slice_in_dim(shocks, start, fac_width, 1)
        load_block = lax.dynamic_slice_in_dim(loading, start, fac_width, 0)
        partial_sum = jnp.dot(shock_block, load_block, preferred_element_type=jnp.float32)
        return running + partial_sum, None

    start_losses = jnp.zeros((SCENARIOS, PORTFOLIOS), jnp.float32)
    losses, unused = lax.scan(add_block, start_losses, jnp.arange(N_FAC, dtype=jnp.int32))
    scen_weights = weights.astype(jnp.float32)

    def level(limit):
        diff = losses - limit[None, :]
        smooth = jax.nn.sigmoid(diff / smooth_width)
        weighted = scen_weights[:, None] * smooth
        return jnp.sum(weighted, axis=0), jnp.sum(weighted * diff, axis=0)

    count, excess = lax.map(level, thresholds)
    total = jnp.sum(scen_weights)
    return excess / jnp.maximum(count, 1.0), count / total
```

```python
import functools

import jax
import jax.numpy as jnp
from jax import lax
from jax.experimental import pallas as pl
from jax.experimental.pallas import tpu as pltpu
from jax.sharding import PartitionSpec as P

smooth_width = 0.05
half_inverse = 0.5 / smooth_width
lane_block = 256
row_block = 256
level_group = 8


def tail_body(count_own, losses, levels, weights, count_in, excess_in, count_out, excess_out):
    rows = losses.shape[0]
    groups = levels.shape[0] // level_group
    bf16 = jnp.bfloat16

    @pl.when(pl.program_id(0) < count_own[0])
    def _():
        which = lax.broadcasted_iota(jnp.int32, (level_group, row_block), 0)

        def group(at, carry):
            span = pl.ds(pl.multiple_of(at * level_group, level_group), level_group)
            limits = levels[span, :]
            count = count_in[span, :]
            excess = excess_in[span, :]
            for start in range(0, rows, row_block):
                row_weights = weights[:, pl.ds(start, row_block)]
                for level in range(level_group):
                    picked = jnp.where(which == level, row_weights, jnp.zeros_like(row_weights))
                    limit = jnp.broadcast_to(limits[level : level + 1, :], (32, lane_block))
                    smooth, products = [], []
                    for row in range(start, start + row_block, 32):
                        diff = (losses[pl.ds(row, 32), :] - limit).astype(bf16)
                        twice = jnp.tanh(diff) + bf16(1)
                        smooth.append(twice)
                        products.append(twice * diff)
                    count = count + jnp.dot(
                        picked, jnp.concatenate(smooth, 0), preferred_element_type=jnp.float32
                    )
                    excess = excess + jnp.dot(
                        picked, jnp.concatenate(products, 0), preferred_element_type=jnp.float32
                    )
            count_out[span, :] = count
            excess_out[span, :] = excess
            return carry

        lax.fori_loop(0, groups, group, 0)


def tail_sums(count_own, losses, levels, weights, count, excess):
    rows, width = losses.shape
    depth = levels.shape[0]
    table = pl.BlockSpec((depth, lane_block), lambda i, own: (0, i))
    return pl.pallas_call(
        tail_body,
        out_shape=[jax.ShapeDtypeStruct((depth, width), jnp.float32)] * 2,
        grid_spec=pltpu.PrefetchScalarGridSpec(
            num_scalar_prefetch=1,
            grid=(width // lane_block,),
            in_specs=[
                pl.BlockSpec((rows, lane_block), lambda i, own: (0, i)),
                table,
                pl.BlockSpec((8, rows), lambda i, own: (0, 0)),
                table,
                table,
            ],
            out_specs=[table, table],
        ),
        input_output_aliases={4: 0, 5: 1},
        cost_estimate=pl.CostEstimate(
            flops=rows * width * depth * 8,
            transcendentals=rows * width * depth,
            bytes_accessed=rows * width * 4 + depth * width * 20,
        ),
        name="tail_sums",
    )(count_own, losses, levels, weights, count, excess)


def pipelined(shocks, loading, thresholds, weights):
    rows = shocks.shape[0]
    width = loading.shape[1]
    half = width // 2
    owned = 3 * half // 4
    link, f32 = jnp.float16, jnp.float32
    place = lax.axis_index("fac")
    at_end = (place == 0) | (place == 3)
    upper = (place >= 2).astype(jnp.int32)

    def exchange_core(v):
        return lax.ppermute(v, "port", [(0, 1), (1, 0), (2, 3), (3, 2)])

    def exchange_chip(v):
        return lax.ppermute(v, "port", [(0, 2), (2, 0), (1, 3), (3, 1)])

    def halves(v, k):
        return lax.dynamic_slice_in_dim(v, k * half, half, 1)

    def own_part(v):
        return jnp.where(at_end, v[:, :owned], jnp.pad(v[:, owned:], ((0, 0), (0, 2 * owned - half))))

    weights_pair = jnp.stack([weights, exchange_core(weights)])
    weights_far = exchange_chip(weights_pair)
    group_total = jnp.sum(weights_pair.astype(f32)) + jnp.sum(weights_far.astype(f32))
    total = group_total + lax.ppermute(group_total, "scen", [(0, 1), (1, 0)])

    piece = rows // 4
    far = []
    for k in range(4):
        got = exchange_chip(shocks[k * piece : (k + 1) * piece])
        far.append((got, exchange_core(got)))
    sibling = exchange_core(shocks)
    blocks = [
        (shocks, weights_pair[0]),
        (sibling, weights_pair[1]),
    ]
    for k in range(4):
        part = slice(k * piece, (k + 1) * piece)
        blocks.append((jnp.concatenate(far[k], 0), weights_far[:, part].reshape(-1)))

    limits = own_part(halves(thresholds, upper)) * half_inverse
    count_own = jnp.where(at_end, owned // lane_block, (half - owned) // lane_block).astype(jnp.int32).reshape(1)
    count = jnp.zeros((limits.shape[0], owned), f32)
    excess = jnp.zeros((limits.shape[0], owned), f32)
    for block, block_weights in blocks:
        partial = (jnp.dot(block, loading, preferred_element_type=f32) * half_inverse).astype(link)
        away = halves(partial, 1 - upper)
        near = halves(partial, upper)
        first = lax.ppermute(
            jnp.concatenate([away, near[:, owned:]], 1), "fac", [(0, 1), (3, 2)]
        )
        passed = (away.astype(f32) + first[:, :half].astype(f32)).astype(link)
        second = lax.ppermute(passed, "fac", [(1, 2), (2, 1)])
        near = near.astype(f32) + second.astype(f32)
        third = lax.ppermute(near[:, :owned].astype(link), "fac", [(1, 0), (2, 3)])
        losses = own_part(near) + jnp.where(
            at_end,
            third,
            jnp.pad(first[:, half:], ((0, 0), (0, 2 * owned - half))),
        ).astype(f32)
        spread = jnp.broadcast_to(block_weights[None], (8, block_weights.shape[0]))
        count, excess = tail_sums(count_own, losses, limits, spread, count, excess)

    sums = jnp.concatenate([count * 0.5, excess * (0.5 / half_inverse)], 0)
    sums = sums + lax.ppermute(sums, "scen", [(0, 1), (1, 0)])
    depth = limits.shape[0]
    count, excess = sums[:depth], sums[depth:]
    result = jnp.concatenate([excess / jnp.maximum(count, 1.0), count / total], 0)
    ends = [result] + [
        lax.ppermute(result, "fac", pairs)
        for pairs in ([(0, 1), (3, 2)], [(0, 2), (3, 1)], [(0, 3), (3, 0)])
    ]
    inner = result[:, : half - owned]
    mids = [inner] + [
        lax.ppermute(inner, "fac", pairs)
        for pairs in ([(1, 0), (2, 3)], [(1, 2), (2, 1)], [(1, 3), (2, 0)])
    ]

    def choose(parts, order):
        out = parts[order[3]]
        for k in (2, 1, 0):
            out = jnp.where(place == k, parts[order[k]], out)
        return out

    full = jnp.concatenate(
        [
            choose(ends, (0, 1, 2, 3)),
            choose(mids, (1, 0, 2, 3)),
            choose(ends, (3, 2, 1, 0)),
            choose(mids, (3, 2, 0, 1)),
        ],
        1,
    )
    return full[:depth], full[depth:]


def sums_rows(losses, levels, scen_weights):
    width = levels.shape[1]

    def block(limits):
        diff = losses[None, :, :] - limits[:, None, :]
        weighted = scen_weights[None, :, None] * jax.nn.sigmoid(diff / smooth_width)
        return (jnp.sum(weighted, axis=1), jnp.sum(weighted * diff, axis=1))

    count, excess = lax.map(block, levels.reshape(-1, 8, width))
    return (count.reshape(-1, width), excess.reshape(-1, width))


def plain(shocks, loading, thresholds, weights):
    fac_count = lax.axis_size("fac")
    fac_index = lax.axis_index("fac")
    gathered, group_weights = (
        lax.all_gather(shocks, "port", axis=0, tiled=True),
        lax.all_gather(weights, "port", axis=0, tiled=True),
    )
    local_rows = gathered.shape[0] // fac_count
    losses = lax.psum_scatter(
        jnp.dot(gathered, loading, preferred_element_type=jnp.float32),
        "fac",
        scatter_dimension=0,
        tiled=True,
    )
    own_weights = lax.dynamic_slice_in_dim(
        group_weights, fac_index * local_rows, local_rows, 0
    ).astype(jnp.float32)
    count, excess = sums_rows(losses, thresholds, own_weights)
    count, excess, total = lax.psum((count, excess, jnp.sum(own_weights)), ("fac", "scen"))
    return (excess / jnp.maximum(count, 1.0), count / total)


def per_device(shocks, loading, thresholds, weights):
    sizes = tuple(lax.axis_size(name) for name in ("port", "fac", "scen"))
    fits = (
        sizes == (4, 4, 2)
        and shocks.shape[0] % 512 == 0
        and loading.shape[1] % 2048 == 0
        and thresholds.shape[0] % level_group == 0
    )
    if fits:
        return pipelined(shocks, loading, thresholds, weights)
    return plain(shocks, loading, thresholds, weights)


def solution(mesh):
    placed = (P(("port", "scen"), "fac"), P("fac", "port"), P(None, "port"), P(("port", "scen")))
    return jax.shard_map(
        per_device,
        mesh=mesh,
        in_specs=placed,
        out_specs=(P(None, "port"), P(None, "port")),
        check_vma=False,
    )
```

```python
import functools

import jax
import jax.numpy as jnp
from jax import lax
from jax.experimental import pallas as pl
from jax.experimental.pallas import tpu as pltpu
from jax.sharding import PartitionSpec as P

smooth_width = 0.05
half_inverse = 0.5 / smooth_width
lane_block = 256
row_block = 256
level_group = 8


def tail_body(losses, levels, weights, count_in, excess_in, count_out, excess_out):
    rows = losses.shape[0]
    bf16 = jnp.bfloat16
    which = lax.broadcasted_iota(jnp.int32, (level_group, row_block), 0)

    def group(at, carry):
        span = pl.ds(pl.multiple_of(at * level_group, level_group), level_group)
        limits = levels[span, :]
        count = count_in[span, :]
        excess = excess_in[span, :]
        for start in range(0, rows, row_block):
            row_weights = weights[:, pl.ds(start, row_block)]
            for level in range(level_group):
                picked = jnp.where(which == level, row_weights, jnp.zeros_like(row_weights))
                limit = jnp.broadcast_to(limits[level : level + 1, :], (32, lane_block))
                smooth, products = [], []
                for row in range(start, start + row_block, 32):
                    diff = (losses[pl.ds(row, 32), :] - limit).astype(bf16)
                    twice = jnp.tanh(diff) + bf16(1)
                    smooth.append(twice)
                    products.append(twice * diff)
                count = count + jnp.dot(
                    picked, jnp.concatenate(smooth, 0), preferred_element_type=jnp.float32
                )
                excess = excess + jnp.dot(
                    picked, jnp.concatenate(products, 0), preferred_element_type=jnp.float32
                )
        count_out[span, :] = count
        excess_out[span, :] = excess
        return carry

    lax.fori_loop(0, levels.shape[0] // level_group, group, 0)


def tail_sums(losses, levels, weights, count, excess):
    rows, width = losses.shape
    depth = levels.shape[0]
    table = pl.BlockSpec((depth, lane_block), lambda i: (0, i))
    return pl.pallas_call(
        tail_body,
        out_shape=[jax.ShapeDtypeStruct((depth, width), jnp.float32)] * 2,
        grid=(width // lane_block,),
        in_specs=[
            pl.BlockSpec((rows, lane_block), lambda i: (0, i)),
            table,
            pl.BlockSpec((8, rows), lambda i: (0, 0)),
            table,
            table,
        ],
        out_specs=[table, table],
        input_output_aliases={3: 0, 4: 1},
        cost_estimate=pl.CostEstimate(flops=1024, transcendentals=0, bytes_accessed=1024),
        name="tail_sums",
    )(losses, levels, weights, count, excess)


def together(*values):
    return lax.optimization_barrier(values)


def pipelined(shocks, loading, thresholds, weights):
    rows = shocks.shape[0]
    quarter = loading.shape[1] // 4
    link, f32 = jnp.float16, jnp.float32
    place = lax.axis_index("fac")
    low, high = place % 2, place // 2

    def swap(v, axis, flip):
        return lax.ppermute(v, axis, [(i, i ^ flip) for i in range(lax.axis_size(axis))])

    def columns(v, k, width):
        return lax.dynamic_slice_in_dim(v, k * width, width, 1)

    def product(block):
        return (jnp.dot(block, loading, preferred_element_type=f32) * half_inverse).astype(link)

    def send_a(partial):
        return columns(partial, 1 - low, 2 * quarter)

    def send_b(partial, got):
        at = 2 * low + 1 - high
        return (columns(partial, at, quarter).astype(f32) + columns(got, 1 - high, quarter).astype(f32)).astype(link)

    def finish(partial, got, last):
        at = 2 * low + high
        return (
            columns(partial, at, quarter).astype(f32)
            + columns(got, high, quarter).astype(f32)
            + last.astype(f32)
        )

    split = rows // 2
    limits = columns(thresholds, 2 * low + high, quarter) * half_inverse
    zero = jnp.zeros(limits.shape, f32)

    weights_pair = jnp.stack([weights, swap(weights, "port", 1)])
    weights_far = swap(weights_pair, "port", 2)
    group_total = jnp.sum(weights_pair.astype(f32)) + jnp.sum(weights_far.astype(f32))
    total = group_total + swap(group_total, "scen", 1)
    block_weights = [
        weights_pair[0],
        weights_pair[1],
        weights_far[:, :split].reshape(-1),
        weights_far[:, split:].reshape(-1),
    ]

    def tails(losses, which, sums):
        w = block_weights[which]
        return tail_sums(losses, limits, jnp.broadcast_to(w[None], (8, w.shape[0])), *sums)

    sums = (zero, zero)
    far0 = swap(shocks[:split], "port", 2)
    sibling = swap(shocks, "port", 1)
    p0 = product(shocks)
    a0, sibling, p0 = together(send_a(p0), sibling, p0)

    a0 = swap(a0, "fac", 1)
    p1 = product(sibling)
    a0, p1, far0 = together(a0, p1, far0)

    b0, a1, far0, far1 = together(send_b(p0, a0), send_a(p1), far0, shocks[split:])
    a1 = swap(a1, "fac", 1)
    b0 = swap(b0, "fac", 2)
    far1 = swap(far1, "port", 2)
    p2 = product(jnp.concatenate([far0, swap(far0, "port", 1)], 0))
    a1, b0, p2, far1 = together(a1, b0, p2, far1)

    b1, a2, far1, done = together(send_b(p1, a1), send_a(p2), far1, finish(p0, a0, b0))
    a2 = swap(a2, "fac", 1)
    b1 = swap(b1, "fac", 2)
    p3 = product(jnp.concatenate([far1, swap(far1, "port", 1)], 0))
    sums = tails(together(done, p3)[0], 0, sums)
    a2, b1, p3, sums = together(a2, b1, p3, sums)

    b2, a3, done, sums = together(send_b(p2, a2), send_a(p3), finish(p1, a1, b1), sums)
    a3 = swap(a3, "fac", 1)
    b2 = swap(b2, "fac", 2)
    sums = tails(done, 1, sums)
    a3, b2, sums = together(a3, b2, sums)

    b3, done, sums = together(send_b(p3, a3), finish(p2, a2, b2), sums)
    b3 = swap(b3, "fac", 2)
    sums = tails(done, 2, sums)
    b3, sums = together(b3, sums)
    count, excess = tails(finish(p3, a3, b3), 3, sums)

    sums = jnp.concatenate([count * 0.5, excess * (0.5 / half_inverse)], 0)
    sums = sums + swap(sums, "scen", 1)
    depth = limits.shape[0]
    count, excess = sums[:depth], sums[depth:]
    result = jnp.concatenate([excess / jnp.maximum(count, 1.0), count / total], 0)
    parts = [result] + [swap(result, "fac", flip) for flip in (1, 2, 3)]

    def owner(k):
        out = parts[k ^ 3]
        for mine in (2, 1, 0):
            out = jnp.where(place == mine, parts[k ^ mine], out)
        return out

    full = jnp.concatenate([owner(k) for k in (0, 2, 1, 3)], 1)
    return full[:depth], full[depth:]


def sums_rows(losses, levels, scen_weights):
    width = levels.shape[1]

    def block(limits):
        diff = losses[None, :, :] - limits[:, None, :]
        weighted = scen_weights[None, :, None] * jax.nn.sigmoid(diff / smooth_width)
        return (jnp.sum(weighted, axis=1), jnp.sum(weighted * diff, axis=1))

    count, excess = lax.map(block, levels.reshape(-1, 8, width))
    return (count.reshape(-1, width), excess.reshape(-1, width))


def plain(shocks, loading, thresholds, weights):
    fac_count = lax.axis_size("fac")
    fac_index = lax.axis_index("fac")
    gathered, group_weights = (
        lax.all_gather(shocks, "port", axis=0, tiled=True),
        lax.all_gather(weights, "port", axis=0, tiled=True),
    )
    local_rows = gathered.shape[0] // fac_count
    losses = lax.psum_scatter(
        jnp.dot(gathered, loading, preferred_element_type=jnp.float32),
        "fac",
        scatter_dimension=0,
        tiled=True,
    )
    own_weights = lax.dynamic_slice_in_dim(
        group_weights, fac_index * local_rows, local_rows, 0
    ).astype(jnp.float32)
    count, excess = sums_rows(losses, thresholds, own_weights)
    count, excess, total = lax.psum((count, excess, jnp.sum(own_weights)), ("fac", "scen"))
    return (excess / jnp.maximum(count, 1.0), count / total)


def per_device(shocks, loading, thresholds, weights):
    sizes = tuple(lax.axis_size(name) for name in ("port", "fac", "scen"))
    fits = (
        sizes == (4, 4, 2)
        and shocks.shape[0] % 512 == 0
        and loading.shape[1] % 2048 == 0
        and thresholds.shape[0] % level_group == 0
    )
    if fits:
        return pipelined(shocks, loading, thresholds, weights)
    return plain(shocks, loading, thresholds, weights)


def solution(mesh):
    placed = (P(("port", "scen"), "fac"), P("fac", "port"), P(None, "port"), P(("port", "scen")))
    return jax.shard_map(
        per_device,
        mesh=mesh,
        in_specs=placed,
        out_specs=(P(None, "port"), P(None, "port")),
        check_vma=False,
    )
```

```python
import functools

import jax
import jax.numpy as jnp
from jax import lax
from jax.experimental import pallas as pl
from jax.experimental.pallas import tpu as pltpu
from jax.sharding import PartitionSpec as P

smooth_width = 0.05
half_inverse = 0.5 / smooth_width
lane_block = 256
level_group = 8


def tail_body(losses, levels, weights, sums_in, sums_out):
    rows = losses.shape[0]
    row_block = rows if rows <= 512 else 32
    depth = levels.shape[0]
    bf16 = jnp.bfloat16
    which = lax.broadcasted_iota(jnp.int32, (level_group, row_block), 0)

    def group(at, carry):
        span = pl.ds(pl.multiple_of(at * level_group, level_group), level_group)
        limits = levels[span, :]
        second = pl.ds(pl.multiple_of(depth + at * level_group, level_group), level_group)
        count = sums_in[span, :]
        excess = sums_in[second, :]
        for start in range(0, rows, row_block):
            row_weights = weights[:, pl.ds(start, row_block)]
            for level in range(level_group):
                picked = jnp.where(which == level, row_weights, jnp.zeros_like(row_weights))
                limit = jnp.broadcast_to(limits[level : level + 1, :], (32, lane_block))
                smooth, products = [], []
                for row in range(start, start + row_block, 32):
                    diff = losses[pl.ds(row, 32), :] - limit
                    twice = (jnp.tanh(diff) + 1.0).astype(bf16)
                    smooth.append(twice)
                    products.append(twice * diff.astype(bf16))
                count = count + jnp.dot(
                    picked, jnp.concatenate(smooth, 0), preferred_element_type=jnp.float32
                )
                excess = excess + jnp.dot(
                    picked, jnp.concatenate(products, 0), preferred_element_type=jnp.float32
                )
        sums_out[span, :] = count
        sums_out[second, :] = excess
        return carry

    lax.fori_loop(0, depth // level_group, group, 0)


def tail_sums(losses, levels, weights, sums):
    rows, width = losses.shape
    depth = levels.shape[0]
    both = pl.BlockSpec((2 * depth, lane_block), lambda i: (0, i))
    return pl.pallas_call(
        tail_body,
        out_shape=jax.ShapeDtypeStruct((2 * depth, width), jnp.float32),
        grid=(width // lane_block,),
        in_specs=[
            pl.BlockSpec((rows, lane_block), lambda i: (0, i)),
            pl.BlockSpec((depth, lane_block), lambda i: (0, i)),
            pl.BlockSpec((8, rows), lambda i: (0, 0)),
            both,
        ],
        out_specs=both,
        input_output_aliases={3: 0},
        cost_estimate=pl.CostEstimate(flops=1024, transcendentals=0, bytes_accessed=1024),
        name="tail_sums",
    )(losses, levels, weights, sums)


def together(*values):
    return lax.optimization_barrier(values)


def pipelined(shocks, loading, thresholds, weights):
    rows = shocks.shape[0]
    quarter = loading.shape[1] // 4
    link, f32 = jnp.float16, jnp.float32
    place = lax.axis_index("fac")
    low, high = place % 2, place // 2

    def swap(v, axis, flip):
        return lax.ppermute(v, axis, [(i, i ^ flip) for i in range(lax.axis_size(axis))])

    def columns(v, k, width):
        return lax.dynamic_slice_in_dim(v, k * width, width, 1)

    def product(block):
        return (jnp.dot(block, loading, preferred_element_type=f32) * half_inverse).astype(link)

    def send_a(partial):
        return columns(partial, 1 - low, 2 * quarter)

    def send_b(partial, got):
        at = 2 * low + 1 - high
        return (columns(partial, at, quarter).astype(f32) + columns(got, 1 - high, quarter).astype(f32)).astype(link)

    def finish(partial, got, last):
        at = 2 * low + high
        return (
            columns(partial, at, quarter).astype(f32)
            + columns(got, high, quarter).astype(f32)
            + last.astype(f32)
        )

    cuts = [0] + [rows * c // 32 for c in (13, 24)] + [rows]
    pieces = [slice(i, j) for i, j in zip(cuts, cuts[1:])]
    limits = columns(thresholds, 2 * low + high, quarter) * half_inverse
    depth = limits.shape[0]

    blocks = 2 + len(pieces)
    partial, got, last = {}, {}, {}
    sums = jnp.zeros((2 * depth, quarter), f32)
    coming = swap(shocks[pieces[0]], "port", 2)
    sibling = swap(shocks, "port", 1)
    first = product(shocks)
    to_a, sibling, partial[0] = together(send_a(first), sibling, first)

    for step in range(blocks + 1):
        if step < blocks:
            got[step] = swap(to_a, "fac", 1)
        if step > 0:
            last[step - 1] = swap(to_b, "fac", 2)
        nearest = None
        if 1 <= step < len(pieces):
            nearest = swap(to_far, "port", 2)
        if step == 0:
            partial[1] = product(sibling)
            later = together(shocks, partial[1])[0]
            to_fars = {k: later[piece] for k, piece in enumerate(pieces) if k}
        elif step + 1 < blocks:
            partial[step + 1] = product(jnp.concatenate([coming, swap(coming, "port", 1)], 0))
        if step > 1:
            if step + 1 < blocks:
                done = together(done, partial[step + 1])[0]
            sums = tail_sums(done, limits, block_weights[step - 2], sums)
        if step == 0:
            nearest = coming
            pair = jnp.stack([weights, swap(weights, "port", 1)])
            small = (pair, limits)
        elif step == 1:
            small = swap(pair, "port", 2)
        elif step == 2:
            small = swap(group_total, "scen", 1)
        else:
            small = None
        got, last, partial, nearest, sums, to_fars, small = together(
            got, last, partial, nearest, sums, to_fars, small
        )
        if step == 0:
            pair, limits = small
        elif step == 1:
            group_total = jnp.sum(pair.astype(f32)) + jnp.sum(small.astype(f32))
            block_weights = [pair[0], pair[1]]
            block_weights += [small[:, piece].reshape(-1) for piece in pieces]
            block_weights = [jnp.broadcast_to(w[None], (8, w.shape[0])) for w in block_weights]
        elif step == 2:
            total = group_total + small
        coming = nearest
        if step < blocks:
            to_b = send_b(partial[step], got[step])
        if step + 1 < blocks:
            to_a = send_a(partial[step + 1])
        if step + 1 < len(pieces):
            to_far = to_fars[step + 1]
        else:
            to_far = None
        if step > 0:
            done = finish(partial[step - 1], got[step - 1], last[step - 1])
        else:
            done = None
        to_a, to_b, to_far, coming, done, sums = together(to_a, to_b, to_far, coming, done, sums)
    sums = tail_sums(done, limits, block_weights[blocks - 1], sums)

    sums = sums + swap(sums, "scen", 1)
    count, excess = sums[:depth] * 0.5, sums[depth:] * (0.5 / half_inverse)
    result = jnp.concatenate([excess / jnp.maximum(count, 1.0), count / total], 0)
    parts = [result] + [swap(result, "fac", flip) for flip in (1, 2, 3)]

    def owner(k):
        out = parts[k ^ 3]
        for mine in (2, 1, 0):
            out = jnp.where(place == mine, parts[k ^ mine], out)
        return out

    full = jnp.concatenate([owner(k) for k in (0, 2, 1, 3)], 1)
    return full[:depth], full[depth:]


def sums_rows(losses, levels, scen_weights):
    width = levels.shape[1]

    def block(limits):
        diff = losses[None, :, :] - limits[:, None, :]
        weighted = scen_weights[None, :, None] * jax.nn.sigmoid(diff / smooth_width)
        return (jnp.sum(weighted, axis=1), jnp.sum(weighted * diff, axis=1))

    count, excess = lax.map(block, levels.reshape(-1, 8, width))
    return (count.reshape(-1, width), excess.reshape(-1, width))


def plain(shocks, loading, thresholds, weights):
    fac_count = lax.axis_size("fac")
    fac_index = lax.axis_index("fac")
    gathered, group_weights = (
        lax.all_gather(shocks, "port", axis=0, tiled=True),
        lax.all_gather(weights, "port", axis=0, tiled=True),
    )
    local_rows = gathered.shape[0] // fac_count
    losses = lax.psum_scatter(
        jnp.dot(gathered, loading, preferred_element_type=jnp.float32),
        "fac",
        scatter_dimension=0,
        tiled=True,
    )
    own_weights = lax.dynamic_slice_in_dim(
        group_weights, fac_index * local_rows, local_rows, 0
    ).astype(jnp.float32)
    count, excess = sums_rows(losses, thresholds, own_weights)
    count, excess, total = lax.psum((count, excess, jnp.sum(own_weights)), ("fac", "scen"))
    return (excess / jnp.maximum(count, 1.0), count / total)


def per_device(shocks, loading, thresholds, weights):
    sizes = tuple(lax.axis_size(name) for name in ("port", "fac", "scen"))
    fits = (
        sizes == (4, 4, 2)
        and shocks.shape[0] % 512 == 0
        and loading.shape[1] % 2048 == 0
        and thresholds.shape[0] % level_group == 0
    )
    if fits:
        return pipelined(shocks, loading, thresholds, weights)
    return plain(shocks, loading, thresholds, weights)


def solution(mesh):
    placed = (P(("port", "scen"), "fac"), P("fac", "port"), P(None, "port"), P(("port", "scen")))
    return jax.shard_map(
        per_device,
        mesh=mesh,
        in_specs=placed,
        out_specs=(P(None, "port"), P(None, "port")),
        check_vma=False,
    )
```

```python
import functools

import jax
import jax.numpy as jnp
from jax import lax
from jax.experimental import pallas as pl
from jax.experimental.pallas import tpu as pltpu
from jax.sharding import PartitionSpec as P

smooth_width = 0.05
half_inverse = 0.5 / smooth_width
lane_block = 256
level_group = 8


def tail_body(first, losses, levels, weights, sums_in, sums_out):
    rows = losses.shape[0]
    row_block = rows if rows <= 512 else 32
    depth = levels.shape[0]
    bf16 = jnp.bfloat16
    which = lax.broadcasted_iota(jnp.int32, (level_group, row_block), 0)

    def group(at, carry):
        span = pl.ds(pl.multiple_of(at * level_group, level_group), level_group)
        limits = levels[span, :]
        second = pl.ds(pl.multiple_of(depth + at * level_group, level_group), level_group)
        count = sums_in[span, :]
        excess = sums_in[second, :]
        for start in range(0, rows, row_block):
            row_weights = weights[:, pl.ds(first + start, row_block)]
            for level in range(level_group):
                picked = jnp.where(which == level, row_weights, jnp.zeros_like(row_weights))
                limit = jnp.broadcast_to(limits[level : level + 1, :], (32, lane_block))
                smooth, products = [], []
                for row in range(start, start + row_block, 32):
                    diff = losses[pl.ds(row, 32), :] - limit
                    twice = (jnp.tanh(diff) + 1.0).astype(bf16)
                    smooth.append(twice)
                    products.append(twice * diff.astype(bf16))
                count = count + jnp.dot(
                    picked, jnp.concatenate(smooth, 0), preferred_element_type=jnp.float32
                )
                excess = excess + jnp.dot(
                    picked, jnp.concatenate(products, 0), preferred_element_type=jnp.float32
                )
        sums_out[span, :] = count
        sums_out[second, :] = excess
        return carry

    sums_out[pl.ds(2 * depth, 8), :] = sums_in[pl.ds(2 * depth, 8), :]
    lax.fori_loop(0, depth // level_group, group, 0, unroll=4)


def tail_sums(losses, levels, weights, first, sums):
    rows, width = losses.shape
    depth = levels.shape[0]
    both = pl.BlockSpec((2 * depth + 8, lane_block), lambda i: (0, i))
    return pl.pallas_call(
        functools.partial(tail_body, first),
        out_shape=jax.ShapeDtypeStruct((2 * depth + 8, width), jnp.float32),
        grid=(width // lane_block,),
        in_specs=[
            pl.BlockSpec((rows, lane_block), lambda i: (0, i)),
            pl.BlockSpec((depth, lane_block), lambda i: (0, i)),
            pl.BlockSpec(weights.shape, lambda i: (0, 0)),
            both,
        ],
        out_specs=both,
        input_output_aliases={3: 0},
        cost_estimate=pl.CostEstimate(flops=1024, transcendentals=0, bytes_accessed=1024),
        name="tail_sums",
    )(losses, levels, weights, sums)


def together(*values):
    return lax.optimization_barrier(values)


def pipelined(shocks, loading, thresholds, weights):
    rows = shocks.shape[0]
    quarter = loading.shape[1] // 4
    link, f32 = jnp.float16, jnp.float32
    place = lax.axis_index("fac")
    low, high = place % 2, place // 2

    def swap(v, axis, flip):
        return lax.ppermute(v, axis, [(i, i ^ flip) for i in range(lax.axis_size(axis))])

    def columns(v, k, width):
        return lax.dynamic_slice_in_dim(v, k * width, width, 1)

    def product(block):
        return (jnp.dot(block, loading, preferred_element_type=f32) * half_inverse).astype(link)

    def send_a(partial):
        return columns(partial, 1 - low, 2 * quarter)

    def send_b(partial, got):
        at = 2 * low + 1 - high
        return (columns(partial, at, quarter).astype(f32) + columns(got, 1 - high, quarter).astype(f32)).astype(link)

    def finish(partial, got, last):
        at = 2 * low + high
        return (
            columns(partial, at, quarter).astype(f32)
            + columns(got, high, quarter).astype(f32)
            + last.astype(f32)
        )

    cuts = [0] + [rows * c // 32 for c in (13, 25)] + [rows]
    pieces = [slice(i, j) for i, j in zip(cuts, cuts[1:])]
    depth = thresholds.shape[0]

    blocks = 2 + len(pieces)
    partial, got, last = {}, {}, {}
    starts = [0, rows] + [2 * rows + 2 * cut for cut in cuts[:-1]]
    sums = None
    coming = swap(shocks[pieces[0]], "port", 2)
    sibling = swap(shocks, "port", 1)
    first = product(shocks)
    to_a, sibling, partial[0] = together(send_a(first), sibling, first)

    for step in range(blocks + 1):
        if step < blocks:
            got[step] = swap(to_a, "fac", 1)
        if step > 0:
            last[step - 1] = swap(to_b, "fac", 2)
        nearest = None
        if 1 <= step < len(pieces):
            nearest = swap(to_far, "port", 2)
        if step == 0:
            partial[1] = product(sibling)
            later = together(shocks, partial[1])[0]
            to_fars = {k: later[piece] for k, piece in enumerate(pieces) if k}
        elif step + 1 < blocks:
            partial[step + 1] = product(jnp.concatenate([coming, swap(coming, "port", 1)], 0))
        if step > 1:
            k = step - 2
            summed = (partial[k], got[k], last[k], pair, far_weights)
            if step + 1 < blocks:
                summed = together(summed, partial[step + 1])[0]
            *summed, pair, far_weights = summed
            if sums is None:
                group_total = jnp.sum(pair.astype(f32)) + jnp.sum(far_weights.astype(f32))
                parts = [pair.reshape(-1)]
                parts += [far_weights[:, piece].reshape(-1) for piece in pieces]
                row_weights = jnp.broadcast_to(jnp.concatenate(parts)[None], (8, 4 * rows))
                sums = jnp.concatenate(
                    [jnp.zeros((2 * depth, quarter), f32), jnp.full((8, quarter), group_total)], 0
                )
            sums = tail_sums(finish(*summed), limits, row_weights, starts[k], sums)
        if step == 0:
            nearest = coming
            pair = small = jnp.stack([weights, swap(weights, "port", 1)])
        elif step == 1:
            limits = columns(together(thresholds, partial[2])[0], 2 * low + high, quarter)
            small = (swap(pair, "port", 2), limits * half_inverse)
        else:
            small = None
        got, last, partial, nearest, sums, to_fars, small = together(
            got, last, partial, nearest, sums, to_fars, small
        )
        if step == 0:
            pair = small
        elif step == 1:
            far_weights, limits = small
        coming = nearest
        if step < blocks:
            to_b = send_b(partial[step], got[step])
        if step + 1 < blocks:
            to_a = send_a(partial[step + 1])
        if step + 1 < len(pieces):
            to_far = to_fars[step + 1]
        else:
            to_far = None
        to_a, to_b, to_far, coming = together(to_a, to_b, to_far, coming)
    k = blocks - 1
    done = finish(partial[k], got[k], last[k])
    sums = tail_sums(done, limits, row_weights, starts[blocks - 1], sums)

    sums = sums + swap(sums, "scen", 1)
    count, excess = sums[:depth] * 0.5, sums[depth : 2 * depth] * (0.5 / half_inverse)
    total = sums[2 * depth : 2 * depth + 1]
    result = jnp.concatenate([excess / jnp.maximum(count, 1.0), count / total], 0)
    parts = [result] + [swap(result, "fac", flip) for flip in (1, 2, 3)]

    def owner(k):
        out = parts[k ^ 3]
        for mine in (2, 1, 0):
            out = jnp.where(place == mine, parts[k ^ mine], out)
        return out

    full = jnp.concatenate([owner(k) for k in (0, 2, 1, 3)], 1)
    return full[:depth], full[depth:]


def sums_rows(losses, levels, scen_weights):
    width = levels.shape[1]

    def block(limits):
        diff = losses[None, :, :] - limits[:, None, :]
        weighted = scen_weights[None, :, None] * jax.nn.sigmoid(diff / smooth_width)
        return (jnp.sum(weighted, axis=1), jnp.sum(weighted * diff, axis=1))

    count, excess = lax.map(block, levels.reshape(-1, 8, width))
    return (count.reshape(-1, width), excess.reshape(-1, width))


def plain(shocks, loading, thresholds, weights):
    fac_count = lax.axis_size("fac")
    fac_index = lax.axis_index("fac")
    gathered, group_weights = (
        lax.all_gather(shocks, "port", axis=0, tiled=True),
        lax.all_gather(weights, "port", axis=0, tiled=True),
    )
    local_rows = gathered.shape[0] // fac_count
    losses = lax.psum_scatter(
        jnp.dot(gathered, loading, preferred_element_type=jnp.float32),
        "fac",
        scatter_dimension=0,
        tiled=True,
    )
    own_weights = lax.dynamic_slice_in_dim(
        group_weights, fac_index * local_rows, local_rows, 0
    ).astype(jnp.float32)
    count, excess = sums_rows(losses, thresholds, own_weights)
    count, excess, total = lax.psum((count, excess, jnp.sum(own_weights)), ("fac", "scen"))
    return (excess / jnp.maximum(count, 1.0), count / total)


def per_device(shocks, loading, thresholds, weights):
    sizes = tuple(lax.axis_size(name) for name in ("port", "fac", "scen"))
    fits = (
        sizes == (4, 4, 2)
        and shocks.shape[0] % 512 == 0
        and loading.shape[1] % 2048 == 0
        and thresholds.shape[0] % level_group == 0
    )
    if fits:
        return pipelined(shocks, loading, thresholds, weights)
    return plain(shocks, loading, thresholds, weights)


def solution(mesh):
    placed = (P(("port", "scen"), "fac"), P("fac", "port"), P(None, "port"), P(("port", "scen")))
    return jax.shard_map(
        per_device,
        mesh=mesh,
        in_specs=placed,
        out_specs=(P(None, "port"), P(None, "port")),
        check_vma=False,
    )
```

```python
import functools

import jax
import jax.numpy as jnp
from jax import lax
from jax.experimental import pallas as pl
from jax.experimental.pallas import tpu as pltpu
from jax.sharding import PartitionSpec as P

smooth_width = 0.05
half_inverse = 0.5 / smooth_width
lane_block = 256
level_group = 8


def tail_body(first, losses, levels, weights, sums_in, sums_out):
    rows = losses.shape[0]
    row_block = rows if rows <= 512 else 32
    depth = levels.shape[0]
    bf16 = jnp.bfloat16
    which = lax.broadcasted_iota(jnp.int32, (level_group, row_block), 0)

    def group(at, carry):
        span = pl.ds(pl.multiple_of(at * level_group, level_group), level_group)
        limits = levels[span, :]
        second = pl.ds(pl.multiple_of(depth + at * level_group, level_group), level_group)
        count = sums_in[span, :]
        excess = sums_in[second, :]
        for start in range(0, rows, row_block):
            row_weights = weights[:, pl.ds(first + start, row_block)]
            for level in range(level_group):
                picked = jnp.where(which == level, row_weights, jnp.zeros_like(row_weights))
                limit = jnp.broadcast_to(limits[level : level + 1, :], (32, lane_block))
                smooth, products = [], []
                for row in range(start, start + row_block, 32):
                    diff = losses[pl.ds(row, 32), :] - limit
                    twice = (jnp.tanh(diff) + 1.0).astype(bf16)
                    smooth.append(twice)
                    products.append(twice * diff.astype(bf16))
                count = count + jnp.dot(
                    picked, jnp.concatenate(smooth, 0), preferred_element_type=jnp.float32
                )
                excess = excess + jnp.dot(
                    picked, jnp.concatenate(products, 0), preferred_element_type=jnp.float32
                )
        sums_out[span, :] = count
        sums_out[second, :] = excess
        return carry

    sums_out[pl.ds(2 * depth, 8), :] = sums_in[pl.ds(2 * depth, 8), :]
    lax.fori_loop(0, depth // level_group, group, 0, unroll=4)


def tail_sums(losses, levels, weights, first, sums):
    rows, width = losses.shape
    depth = levels.shape[0]
    both = pl.BlockSpec((2 * depth + 8, lane_block), lambda i: (0, i))
    return pl.pallas_call(
        functools.partial(tail_body, first),
        out_shape=jax.ShapeDtypeStruct((2 * depth + 8, width), jnp.float32),
        grid=(width // lane_block,),
        in_specs=[
            pl.BlockSpec((rows, lane_block), lambda i: (0, i)),
            pl.BlockSpec((depth, lane_block), lambda i: (0, i)),
            pl.BlockSpec(weights.shape, lambda i: (0, 0)),
            both,
        ],
        out_specs=both,
        input_output_aliases={3: 0},
        cost_estimate=pl.CostEstimate(flops=1024, transcendentals=0, bytes_accessed=1024),
        name="tail_sums",
    )(losses, levels, weights, sums)


def together(*values):
    return lax.optimization_barrier(values)


def pipelined(shocks, loading, thresholds, weights):
    rows = shocks.shape[0]
    quarter = loading.shape[1] // 4
    link, f32 = jnp.float16, jnp.float32
    place = lax.axis_index("fac")
    low, high = place % 2, place // 2

    def swap(v, axis, flip):
        return lax.ppermute(v, axis, [(i, i ^ flip) for i in range(lax.axis_size(axis))])

    def columns(v, k, width):
        return lax.dynamic_slice_in_dim(v, k * width, width, 1)

    def product(block, factors=loading):
        return (jnp.dot(block, factors, preferred_element_type=f32) * half_inverse).astype(link)

    def kept(partial, k):
        if isinstance(partial, tuple):
            return columns(partial[0], k, quarter)
        return columns(partial, 2 * low + k, quarter)

    def send_a(partial):
        return columns(partial, 1 - low, 2 * quarter)

    def send_b(partial, got):
        return (kept(partial, 1 - high).astype(f32) + columns(got, 1 - high, quarter).astype(f32)).astype(link)

    def finish(partial, got, last):
        return (
            kept(partial, high).astype(f32)
            + columns(got, high, quarter).astype(f32)
            + last.astype(f32)
        )

    cuts = [0] + [rows * c // 32 for c in (12, 24)] + [rows]
    pieces = [slice(i, j) for i, j in zip(cuts, cuts[1:])]
    depth = thresholds.shape[0]

    blocks = 2 + len(pieces)
    partial, got, last = {}, {}, {}
    starts = [0, rows] + [2 * rows + 2 * cut for cut in cuts[:-1]]
    sums = None
    coming = swap(shocks[pieces[0]], "port", 2)
    sibling = swap(shocks, "port", 1)
    first = product(shocks, columns(loading, 1 - low, 2 * quarter))
    to_a, sibling = together(first, sibling)

    for step in range(blocks + 1):
        if step < blocks:
            got[step] = swap(to_a, "fac", 1)
        if step > 0:
            last[step - 1] = swap(to_b, "fac", 2)
        nearest = None
        if 1 <= step < len(pieces):
            nearest = swap(to_far, "port", 2)
        if step == 0:
            partial[0] = (product(shocks, columns(together(loading, to_a)[0], low, 2 * quarter)),)
            partial[1] = product(together(sibling, partial[0][0])[0])
            to_fars = {1: together(shocks, partial[1])[0][pieces[1]]}
        elif step + 1 < blocks:
            partial[step + 1] = product(jnp.concatenate([coming, swap(coming, "port", 1)], 0))
        if step > 1:
            k = step - 2
            summed = (partial[k], got[k], last[k], pair, far_weights)
            if step + 1 < blocks:
                summed = together(summed, partial[step + 1])[0]
            *summed, pair, far_weights = summed
            if sums is None:
                group_total = jnp.sum(pair.astype(f32)) + jnp.sum(far_weights.astype(f32))
                parts = [pair.reshape(-1)]
                parts += [far_weights[:, piece].reshape(-1) for piece in pieces]
                row_weights = jnp.broadcast_to(jnp.concatenate(parts)[None], (8, 4 * rows))
                sums = jnp.concatenate(
                    [jnp.zeros((2 * depth, quarter), f32), jnp.full((8, quarter), group_total)], 0
                )
            sums = tail_sums(finish(*summed), limits, row_weights, starts[k], sums)
        if step == 0:
            nearest = coming
            pair = small = jnp.stack([weights, swap(weights, "port", 1)])
        elif step == 1:
            later = together(shocks, partial[2])[0]
            to_fars = {k: later[piece] for k, piece in enumerate(pieces) if k > 1}
            limits = columns(together(thresholds, partial[2])[0], 2 * low + high, quarter)
            small = (swap(pair, "port", 2), limits * half_inverse)
        else:
            small = None
        got, last, partial, nearest, sums, to_fars, small = together(
            got, last, partial, nearest, sums, to_fars, small
        )
        if step == 0:
            pair = small
        elif step == 1:
            far_weights, limits = small
        coming = nearest
        if step < blocks:
            to_b = send_b(partial[step], got[step])
        if step + 1 < blocks:
            to_a = send_a(partial[step + 1])
        if step + 1 < len(pieces):
            to_far = to_fars[step + 1]
        else:
            to_far = None
        to_a, to_b, to_far, coming = together(to_a, to_b, to_far, coming)
    k = blocks - 1
    done = finish(partial[k], got[k], last[k])
    sums = tail_sums(done, limits, row_weights, starts[blocks - 1], sums)

    sums = sums + swap(sums, "scen", 1)
    count, excess = sums[:depth] * 0.5, sums[depth : 2 * depth] * (0.5 / half_inverse)
    total = sums[2 * depth : 2 * depth + 1]
    result = jnp.concatenate([excess / jnp.maximum(count, 1.0), count / total], 0)
    parts = [result] + [swap(result, "fac", flip) for flip in (1, 2, 3)]

    def owner(k):
        out = parts[k ^ 3]
        for mine in (2, 1, 0):
            out = jnp.where(place == mine, parts[k ^ mine], out)
        return out

    full = jnp.concatenate([owner(k) for k in (0, 2, 1, 3)], 1)
    return full[:depth], full[depth:]


def sums_rows(losses, levels, scen_weights):
    width = levels.shape[1]

    def block(limits):
        diff = losses[None, :, :] - limits[:, None, :]
        weighted = scen_weights[None, :, None] * jax.nn.sigmoid(diff / smooth_width)
        return (jnp.sum(weighted, axis=1), jnp.sum(weighted * diff, axis=1))

    count, excess = lax.map(block, levels.reshape(-1, 8, width))
    return (count.reshape(-1, width), excess.reshape(-1, width))


def plain(shocks, loading, thresholds, weights):
    fac_count = lax.axis_size("fac")
    fac_index = lax.axis_index("fac")
    gathered, group_weights = (
        lax.all_gather(shocks, "port", axis=0, tiled=True),
        lax.all_gather(weights, "port", axis=0, tiled=True),
    )
    local_rows = gathered.shape[0] // fac_count
    losses = lax.psum_scatter(
        jnp.dot(gathered, loading, preferred_element_type=jnp.float32),
        "fac",
        scatter_dimension=0,
        tiled=True,
    )
    own_weights = lax.dynamic_slice_in_dim(
        group_weights, fac_index * local_rows, local_rows, 0
    ).astype(jnp.float32)
    count, excess = sums_rows(losses, thresholds, own_weights)
    count, excess, total = lax.psum((count, excess, jnp.sum(own_weights)), ("fac", "scen"))
    return (excess / jnp.maximum(count, 1.0), count / total)


def per_device(shocks, loading, thresholds, weights):
    sizes = tuple(lax.axis_size(name) for name in ("port", "fac", "scen"))
    fits = (
        sizes == (4, 4, 2)
        and shocks.shape[0] % 512 == 0
        and loading.shape[1] % 2048 == 0
        and thresholds.shape[0] % level_group == 0
    )
    if fits:
        return pipelined(shocks, loading, thresholds, weights)
    return plain(shocks, loading, thresholds, weights)


def solution(mesh):
    placed = (P(("port", "scen"), "fac"), P("fac", "port"), P(None, "port"), P(("port", "scen")))
    return jax.shard_map(
        per_device,
        mesh=mesh,
        in_specs=placed,
        out_specs=(P(None, "port"), P(None, "port")),
        check_vma=False,
    )
```

```python
import functools

import jax
import jax.numpy as jnp
from jax import lax
from jax.experimental import pallas as pl
from jax.experimental.pallas import tpu as pltpu
from jax.sharding import PartitionSpec as P

smooth_width = 0.05
half_inverse = 0.5 / smooth_width
lane_block = 256
level_group = 8


def tail_body(first, losses, levels, weights, sums_in, sums_out):
    rows = losses.shape[0]
    row_block = rows if rows <= 512 else 32
    depth = levels.shape[0]
    bf16 = jnp.bfloat16
    which = lax.broadcasted_iota(jnp.int32, (level_group, row_block), 0)

    def group(at, carry):
        span = pl.ds(pl.multiple_of(at * level_group, level_group), level_group)
        limits = levels[span, :]
        second = pl.ds(pl.multiple_of(depth + at * level_group, level_group), level_group)
        count = sums_in[span, :]
        excess = sums_in[second, :]
        for start in range(0, rows, row_block):
            row_weights = weights[:, pl.ds(first + start, row_block)]
            for level in range(level_group):
                picked = jnp.where(which == level, row_weights, jnp.zeros_like(row_weights))
                limit = jnp.broadcast_to(limits[level : level + 1, :], (32, lane_block))
                smooth, products = [], []
                for row in range(start, start + row_block, 32):
                    diff = losses[pl.ds(row, 32), :] - limit
                    twice = (jnp.tanh(diff) + 1.0).astype(bf16)
                    smooth.append(twice)
                    products.append(twice * diff.astype(bf16))
                count = count + jnp.dot(
                    picked, jnp.concatenate(smooth, 0), preferred_element_type=jnp.float32
                )
                excess = excess + jnp.dot(
                    picked, jnp.concatenate(products, 0), preferred_element_type=jnp.float32
                )
        sums_out[span, :] = count
        sums_out[second, :] = excess
        return carry

    sums_out[pl.ds(2 * depth, 8), :] = sums_in[pl.ds(2 * depth, 8), :]
    lax.fori_loop(0, depth // level_group, group, 0, unroll=4)


def tail_sums(losses, levels, weights, first, sums):
    rows, width = losses.shape
    depth = levels.shape[0]
    both = pl.BlockSpec((2 * depth + 8, lane_block), lambda i: (0, i))
    return pl.pallas_call(
        functools.partial(tail_body, first),
        out_shape=jax.ShapeDtypeStruct((2 * depth + 8, width), jnp.float32),
        grid=(width // lane_block,),
        in_specs=[
            pl.BlockSpec((rows, lane_block), lambda i: (0, i)),
            pl.BlockSpec((depth, lane_block), lambda i: (0, i)),
            pl.BlockSpec(weights.shape, lambda i: (0, 0)),
            both,
        ],
        out_specs=both,
        input_output_aliases={3: 0},
        cost_estimate=pl.CostEstimate(flops=1024, transcendentals=0, bytes_accessed=1024),
        name="tail_sums",
    )(losses, levels, weights, sums)


def together(*values):
    return lax.optimization_barrier(values)


def pipelined(shocks, loading, thresholds, weights):
    rows = shocks.shape[0]
    quarter = loading.shape[1] // 4
    link, f32 = jnp.float16, jnp.float32
    place = lax.axis_index("fac")
    low, high = place % 2, place // 2

    def swap(v, axis, flip):
        return lax.ppermute(v, axis, [(i, i ^ flip) for i in range(lax.axis_size(axis))])

    def columns(v, k, width):
        return lax.dynamic_slice_in_dim(v, k * width, width, 1)

    def product(block, factors=loading):
        return (jnp.dot(block, factors, preferred_element_type=f32) * half_inverse).astype(link)

    def kept(partial, k):
        if isinstance(partial, tuple):
            return columns(partial[0], k, quarter)
        return columns(partial, 2 * low + k, quarter)

    def send_a(partial):
        return columns(partial, 1 - low, 2 * quarter)

    def send_b(partial, got):
        return (kept(partial, 1 - high).astype(f32) + columns(got, 1 - high, quarter).astype(f32)).astype(link)

    def finish(partial, got, last):
        return (
            kept(partial, high).astype(f32)
            + columns(got, high, quarter).astype(f32)
            + last.astype(f32)
        )

    cuts = [0] + [rows * c // 32 for c in (12, 23)] + [rows]
    pieces = [slice(i, j) for i, j in zip(cuts, cuts[1:])]
    depth = thresholds.shape[0]

    blocks = 2 + len(pieces)
    partial, got, last = {}, {}, {}
    starts = [0, rows] + [2 * rows + 2 * cut for cut in cuts[:-1]]
    sums = None
    coming = swap(shocks[pieces[0]], "port", 2)
    sibling = swap(shocks, "port", 1)
    first = product(shocks, columns(loading, 1 - low, 2 * quarter))
    to_a, sibling = together(first, sibling)

    for step in range(blocks + 1):
        if step < blocks:
            got[step] = swap(to_a, "fac", 1)
        if step > 0:
            last[step - 1] = swap(to_b, "fac", 2)
        nearest = None
        if 1 <= step < len(pieces):
            nearest = swap(to_far, "port", 2)
        if step == 0:
            partial[0] = (product(shocks, columns(together(loading, to_a)[0], low, 2 * quarter)),)
            partial[1] = product(together(sibling, partial[0][0])[0])
            to_fars = {1: together(shocks, partial[1])[0][pieces[1]]}
        elif step + 1 < blocks:
            partial[step + 1] = product(jnp.concatenate([coming, swap(coming, "port", 1)], 0))
        if step > 1:
            k = step - 2
            summed = (partial[k], got[k], last[k], pair, far_weights)
            if step + 1 < blocks:
                summed = together(summed, partial[step + 1])[0]
            *summed, pair, far_weights = summed
            if sums is None:
                group_total = jnp.sum(pair.astype(f32)) + jnp.sum(far_weights.astype(f32))
                parts = [pair.reshape(-1)]
                parts += [far_weights[:, piece].reshape(-1) for piece in pieces]
                row_weights = jnp.broadcast_to(jnp.concatenate(parts)[None], (8, 4 * rows))
                sums = jnp.concatenate(
                    [jnp.zeros((2 * depth, quarter), f32), jnp.full((8, quarter), group_total)], 0
                )
            sums = tail_sums(finish(*summed), limits, row_weights, starts[k], sums)
        if step == 0:
            nearest = coming
            pair = small = jnp.stack([weights, swap(weights, "port", 1)])
        elif step == 1:
            later = together(shocks, partial[2])[0]
            to_fars = {k: later[piece] for k, piece in enumerate(pieces) if k > 1}
            limits = columns(together(thresholds, partial[2])[0], 2 * low + high, quarter)
            small = (swap(pair, "port", 2), limits * half_inverse)
        else:
            small = None
        got, last, partial, nearest, sums, to_fars, small = together(
            got, last, partial, nearest, sums, to_fars, small
        )
        if step == 0:
            pair = small
        elif step == 1:
            far_weights, limits = small
        coming = nearest
        if step < blocks:
            to_b = send_b(partial[step], got[step])
        if step + 1 < blocks:
            to_a = send_a(partial[step + 1])
        if step + 1 < len(pieces):
            to_far = to_fars[step + 1]
        else:
            to_far = None
        to_a, to_b, to_far, coming = together(to_a, to_b, to_far, coming)
    k = blocks - 1
    done = finish(partial[k], got[k], last[k])
    sums = tail_sums(done, limits, row_weights, starts[blocks - 1], sums)

    sums = sums + swap(sums, "scen", 1)
    count, excess = sums[:depth] * 0.5, sums[depth : 2 * depth] * (0.5 / half_inverse)
    total = sums[2 * depth : 2 * depth + 1]
    result = jnp.concatenate([excess / jnp.maximum(count, 1.0), count / total], 0)
    parts = [result] + [swap(result, "fac", flip) for flip in (1, 2, 3)]

    def owner(k):
        out = parts[k ^ 3]
        for mine in (2, 1, 0):
            out = jnp.where(place == mine, parts[k ^ mine], out)
        return out

    full = jnp.concatenate([owner(k) for k in (0, 2, 1, 3)], 1)
    return full[:depth], full[depth:]


def sums_rows(losses, levels, scen_weights):
    width = levels.shape[1]

    def block(limits):
        diff = losses[None, :, :] - limits[:, None, :]
        weighted = scen_weights[None, :, None] * jax.nn.sigmoid(diff / smooth_width)
        return (jnp.sum(weighted, axis=1), jnp.sum(weighted * diff, axis=1))

    count, excess = lax.map(block, levels.reshape(-1, 8, width))
    return (count.reshape(-1, width), excess.reshape(-1, width))


def plain(shocks, loading, thresholds, weights):
    fac_count = lax.axis_size("fac")
    fac_index = lax.axis_index("fac")
    gathered, group_weights = (
        lax.all_gather(shocks, "port", axis=0, tiled=True),
        lax.all_gather(weights, "port", axis=0, tiled=True),
    )
    local_rows = gathered.shape[0] // fac_count
    losses = lax.psum_scatter(
        jnp.dot(gathered, loading, preferred_element_type=jnp.float32),
        "fac",
        scatter_dimension=0,
        tiled=True,
    )
    own_weights = lax.dynamic_slice_in_dim(
        group_weights, fac_index * local_rows, local_rows, 0
    ).astype(jnp.float32)
    count, excess = sums_rows(losses, thresholds, own_weights)
    count, excess, total = lax.psum((count, excess, jnp.sum(own_weights)), ("fac", "scen"))
    return (excess / jnp.maximum(count, 1.0), count / total)


def per_device(shocks, loading, thresholds, weights):
    sizes = tuple(lax.axis_size(name) for name in ("port", "fac", "scen"))
    fits = (
        sizes == (4, 4, 2)
        and shocks.shape[0] % 512 == 0
        and loading.shape[1] % 2048 == 0
        and thresholds.shape[0] % level_group == 0
    )
    if fits:
        return pipelined(shocks, loading, thresholds, weights)
    return plain(shocks, loading, thresholds, weights)


def solution(mesh):
    placed = (P(("port", "scen"), "fac"), P("fac", "port"), P(None, "port"), P(("port", "scen")))
    return jax.shard_map(
        per_device,
        mesh=mesh,
        in_specs=placed,
        out_specs=(P(None, "port"), P(None, "port")),
        check_vma=False,
    )
```
